32 devices in a mesh: ctx: 8 (over y, x, core), fsdp: 4 (over z).
Axes of the slice: x: 2, y: 2, z: 4, core: 2. Of those that a mesh axis runs over, the one named last changes fastest.
Arguments:
- layer_in: float32 [4, 1024, 1024], P('fsdp', 'ctx'), may hold values from -6 to 6
- attention_norm_gain: bfloat16 [1024], P('fsdp'), may hold values from 0.5 to 1.5
- attention_norm_bias: bfloat16 [1024], P('fsdp'), may hold values from -1 to 1
- feedforward_norm_gain: bfloat16 [1024], P('fsdp'), may hold values from 0.5 to 1.5
- feedforward_norm_bias: bfloat16 [1024], P('fsdp'), may hold values from -1 to 1
- qkv_weight: bfloat16 [1024, 3072], P('fsdp'), may hold values from -0.1875 to 0.1875
- qkv_bias: bfloat16 [3072], P('fsdp'), may hold values from -2.5 to 2.5
- out_weight: bfloat16 [1024, 1024], P('fsdp'), may hold values from -4 to 4
- out_bias: bfloat16 [1024], P('fsdp'), may hold values from -1 to 1
- fc1_weight: bfloat16 [1024, 4096], P('fsdp'), may hold values from -0.1875 to 0.1875
- fc1_bias: bfloat16 [4096], P('fsdp'), may hold values from -2.5 to 2.5
- fc2_weight: bfloat16 [4096, 1024], P('fsdp'), may hold values from -0.09375 to 0.09375
- fc2_bias: bfloat16 [1024], P('fsdp'), may hold values from -1 to 1
- cotangent: float32 [4, 1024, 1024], P('fsdp', 'ctx'), may hold values from -6 to 6
Outputs:
- layer_out: float32 [4, 1024, 1024], P('fsdp', 'ctx')
- in_grad: float32 [4, 1024, 1024], P('fsdp', 'ctx')
- grad_ln1_gain: float32 [1024], P('fsdp')
- grad_ln1_bias: float32 [1024], P('fsdp')
- grad_ln2_gain: float32 [1024], P('fsdp')
- grad_ln2_bias: float32 [1024], P('fsdp')
- grad_qkv_weight: float32 [1024, 3072], P('fsdp')
- grad_qkv_bias: float32 [3072], P('fsdp')
- grad_out_weight: float32 [1024, 1024], P('fsdp')
- grad_out_bias: float32 [1024], P('fsdp')
- grad_fc1_weight: float32 [1024, 4096], P('fsdp')
- grad_fc1_bias: float32 [4096], P('fsdp')
- grad_fc2_weight: float32 [4096, 1024], P('fsdp')
- grad_fc2_bias: float32 [1024], P('fsdp')
The draws below stay inside these ranges and needn't reach their ends.
All inputs are finite; a program needn't handle non-finite values.
Results may differ from the reference program's by a relative error of at most 0.02.
Values may be sent and summed in bfloat16 or wider, within the bound.
A program may use at most 192 MiB of HBM per device.

```python
import math
import jax
import jax.numpy as jnp
from jax import lax

D = 1024
H = 16
HD = 64
FF = 4096
ROT = 16
TOK_DEV = 128
LENGTH = 1024
SEQS = 4
N_CTX = 8


def levels(own_key, dims, shards, low, high):
    def one(dim, blocks):
        draws = jax.random.uniform(jax.random.fold_in(jax.random.fold_in(own_key, 6), dim), (blocks,), jnp.float32, low / len(shards), high / len(shards))
        return jnp.repeat(jnp.exp(draws), dims[dim] // blocks).reshape((-1,) + (1,) * (len(dims) - dim - 1))

    level = one(*shards[0])
    for cut in shards[1:]:
        level = level * one(*cut)
    return level


def bell_draw(key, dims, deviation, limit, cuts=(), kind=jnp.bfloat16):
    gain = levels(key, dims, cuts, -0.22, 0.18) if cuts else 1.0
    values = jax.random.normal(key, dims, jnp.float32) * deviation * gain
    return jnp.minimum(jnp.maximum(values, -limit), limit).astype(kind)


def setup_inputs(seed: int = 0) -> dict:
    splits = jax.random.split(jax.random.key(seed), 15)
    return {
        "layer_in": bell_draw(splits[0], (SEQS, LENGTH, D), 1.0, 6.0, ((0, 4), (1, 8)), jnp.float32),
        "attention_norm_gain": jnp.clip(1.0 + 0.1 * jax.random.normal(splits[1], (D,), jnp.float32), 0.5, 1.5).astype(jnp.bfloat16),
        "attention_norm_bias": bell_draw(splits[2], (D,), 0.2, 1.0, ((0, 4),)),
        "feedforward_norm_gain": jnp.clip(1.0 + 0.1 * jax.random.normal(splits[3], (D,), jnp.float32), 0.5, 1.5).astype(jnp.bfloat16),
        "feedforward_norm_bias": bell_draw(splits[4], (D,), 0.2, 1.0, ((0, 4),)),
        "qkv_weight": bell_draw(splits[5], (D, 3 * D), D ** -0.5, 0.1875, ((0, 4),)),
        "qkv_bias": bell_draw(splits[6], (3 * D,), 0.5, 2.5, ((0, 4),)),
        "out_weight": bell_draw(splits[7], (D, D), (max(1, 2 * D // LENGTH)) ** -0.5, 4.0, ((0, 4),)),
        "out_bias": bell_draw(splits[8], (D,), 0.2, 1.0, ((0, 4),)),
        "fc1_weight": bell_draw(splits[9], (D, FF), D ** -0.5, 0.1875, ((0, 4),)),
        "fc1_bias": bell_draw(splits[10], (FF,), 0.5, 2.5, ((0, 4),)),
        "fc2_weight": bell_draw(splits[11], (FF, D), FF ** -0.5, 0.09375, ((0, 4),)),
        "fc2_bias": bell_draw(splits[12], (D,), 0.2, 1.0, ((0, 4),)),
        "cotangent": bell_draw(splits[13], (SEQS, LENGTH, D), 1.0, 6.0, ((0, 4), (1, 8)), jnp.float32),
    }


norm_eps = 1e-05
masked_score = -1e+30
root_half = 1.0 / math.sqrt(2.0)
root_two_pi = 1.0 / math.sqrt(2.0 * math.pi)

def widen(array):
    return array.astype(jnp.float32)

def layernorm_forward(values_in, gain_vec, offset):
    centered = values_in - lax.optimization_barrier(jnp.mean(values_in, axis=1, keepdims=True))
    inv_scale = lax.rsqrt(lax.optimization_barrier(jnp.mean(centered * centered, axis=1, keepdims=True)) + norm_eps)
    normed = centered * inv_scale
    return (normed * widen(gain_vec) + widen(offset), normed, inv_scale)

def layernorm_backward(grad_out, normed, inv_scale, gain_vec):
    scaled = grad_out * widen(gain_vec)
    return inv_scale * (scaled - lax.optimization_barrier(jnp.mean(scaled, axis=1, keepdims=True)) - normed * lax.optimization_barrier(jnp.mean(scaled * normed, axis=1, keepdims=True)))

def gelu_value(inputs):
    return 0.5 * inputs * (1.0 + lax.erf(inputs * root_half))

def gelu_slope(inputs):
    return 0.5 * (1.0 + lax.erf(inputs * root_half)) + inputs * jnp.exp(-0.5 * inputs * inputs) * root_two_pi

def angle_tables(positions):
    halfway = ROT // 2
    freqs = jnp.power(10000.0, -2.0 * jnp.arange(halfway, dtype=jnp.float32) / ROT)
    angles = positions.astype(jnp.float32)[:, None] * freqs[None, :]
    return (jnp.cos(angles), jnp.sin(angles))

def split_heads(matrix):
    return matrix.reshape(matrix.shape[0], H, HD)

def rotate_heads(block, cos_table, sin_table):
    halfway = ROT // 2
    leading = block[..., :halfway]
    trailing = block[..., halfway:ROT]
    cos_part = cos_table[:, None, :]
    sin_part = sin_table[:, None, :]
    return jnp.concatenate([leading * cos_part - trailing * sin_part, trailing * cos_part + leading * sin_part, block[..., ROT:]], axis=-1)

def unrotate_heads(block, cos_table, sin_table):
    halfway = ROT // 2
    leading = block[..., :halfway]
    trailing = block[..., halfway:ROT]
    cos_part = cos_table[:, None, :]
    sin_part = sin_table[:, None, :]
    return jnp.concatenate([leading * cos_part + trailing * sin_part, trailing * cos_part - leading * sin_part, block[..., ROT:]], axis=-1)

def block_forward(queries, key_block, value_block, query_pos, key_pos):
    scores = jnp.einsum('qhd,khd->hqk', widen(split_heads(queries)), widen(split_heads(key_block))) * HD ** (-0.5)
    visible = (query_pos[:, None] >= key_pos[None, :])[None]
    scores = jnp.where(visible, scores, masked_score)
    highest = lax.optimization_barrier(jnp.max(scores, axis=2))
    weights = jnp.where(visible, jnp.exp(scores - highest[..., None]), 0.0)
    mixture = jnp.einsum('hqk,khd->hqd', widen(weights.astype(jnp.bfloat16)), widen(split_heads(value_block)))
    return (mixture, highest, lax.optimization_barrier(jnp.sum(weights, axis=2)))

def merge_state(state, update):
    summed, highest, totals = state
    part_sum, part_high, part_total = update
    newest = jnp.maximum(highest, part_high)
    old_factor = jnp.exp(highest - newest)
    new_factor = jnp.exp(part_high - newest)
    return (summed * old_factor[..., None] + part_sum * new_factor[..., None], newest, totals * old_factor + part_total * new_factor)

def block_backward(queries, key_block, value_block, grad_mix, log_total, delta_sum, query_pos, key_pos):
    query_heads = widen(split_heads(queries))
    key_heads = widen(split_heads(key_block))
    value_heads = widen(split_heads(value_block))
    grad_heads = widen(split_heads(grad_mix))
    scores = jnp.einsum('qhd,khd->hqk', query_heads, key_heads) * HD ** (-0.5)
    visible = (query_pos[:, None] >= key_pos[None, :])[None]
    probs = jnp.where(visible, jnp.exp(jnp.where(visible, scores, masked_score) - log_total[..., None]), 0.0)
    value_grad = jnp.einsum('hqk,qhd->khd', widen(probs.astype(jnp.bfloat16)), grad_heads)
    prob_grad = jnp.einsum('qhd,khd->hqk', grad_heads, value_heads)
    score_grad = widen((probs * (prob_grad - delta_sum[..., None]) * HD ** (-0.5)).astype(jnp.bfloat16))
    query_grad = jnp.einsum('hqk,khd->qhd', score_grad, key_heads)
    key_grad = jnp.einsum('hqk,qhd->khd', score_grad, query_heads)
    count = queries.shape[0]
    return (query_grad.reshape(count, H * HD), key_grad.reshape(count, H * HD), value_grad.reshape(count, H * HD))

def reference(layer_in, attention_norm_gain, attention_norm_bias, feedforward_norm_gain, feedforward_norm_bias, qkv_weight, qkv_bias, out_weight, out_bias, fc1_weight, fc1_bias, fc2_weight, fc2_bias, cotangent):
    params = (attention_norm_gain, attention_norm_bias, feedforward_norm_gain, feedforward_norm_bias, qkv_weight, qkv_bias, out_weight, out_bias, fc1_weight, fc1_bias, fc2_weight, fc2_bias)
    offsets = jnp.arange(TOK_DEV, dtype=jnp.int32)
    block_ids = jnp.arange(N_CTX, dtype=jnp.int32)
    half_type = jnp.bfloat16

    def sequence(grad_sums, item):
        incoming_tokens, gradient_token_rows = item
        positions = jnp.arange(LENGTH, dtype=jnp.int32)
        cos_table, sin_table = angle_tables(positions)
        attention_normed_input, attention_standardized, attention_inverse_spread = layernorm_forward(incoming_tokens, attention_norm_gain, attention_norm_bias)
        hidden1 = attention_normed_input.astype(half_type)
        feedforward_normed_input, feedforward_standardized, feedforward_inverse_spread = layernorm_forward(incoming_tokens, feedforward_norm_gain, feedforward_norm_bias)
        hidden2 = feedforward_normed_input.astype(half_type)
        projected = jnp.dot(hidden1, qkv_weight, preferred_element_type=jnp.float32) + widen(qkv_bias)
        queries = rotate_heads(split_heads(projected[:, :D]), cos_table, sin_table).reshape(LENGTH, D).astype(half_type)
        keys_all = rotate_heads(split_heads(projected[:, D:2 * D]), cos_table, sin_table).reshape(LENGTH, D).astype(half_type)
        values_all = projected[:, 2 * D:].astype(half_type)
        query_blocks = queries.reshape(N_CTX, TOK_DEV, D)
        key_blocks = keys_all.reshape(N_CTX, TOK_DEV, D)
        value_blocks = values_all.reshape(N_CTX, TOK_DEV, D)

        def attend(index):
            query_pos = index * TOK_DEV + offsets

            def visit(state, other):
                key_pos = other * TOK_DEV + offsets

                def take(current):
                    return merge_state(current, block_forward(query_blocks[index], key_blocks[other], value_blocks[other], query_pos, key_pos))
                return (lax.cond(other <= index, take, lambda current: current, state), None)
            start_state = (jnp.zeros((H, TOK_DEV, HD), jnp.float32), jnp.full((H, TOK_DEV), masked_score, jnp.float32), jnp.zeros((H, TOK_DEV), jnp.float32))
            final_state, unused = lax.scan(visit, start_state, block_ids)
            summed, highest, totals = final_state
            return ((summed / totals[..., None]).transpose(1, 0, 2).reshape(TOK_DEV, D), highest + jnp.log(totals))
        mixed_rows, log_totals = lax.map(attend, block_ids)
        mixed_heads = mixed_rows.reshape(LENGTH, D).astype(half_type)
        attn_out = jnp.dot(mixed_heads, out_weight, preferred_element_type=jnp.float32) + widen(out_bias)
        pre_act = jnp.dot(hidden2, fc1_weight, preferred_element_type=jnp.float32) + widen(fc1_bias)
        activation = gelu_value(pre_act).astype(half_type)
        layer_rows = incoming_tokens + attn_out + jnp.dot(activation, fc2_weight, preferred_element_type=jnp.float32) + widen(fc2_bias)
        grad_half = gradient_token_rows.astype(half_type)
        grad_mixed = jnp.dot(grad_half, out_weight.T, preferred_element_type=jnp.float32).astype(half_type)
        delta_rows = lax.optimization_barrier(jnp.sum(split_heads(widen(grad_mixed) * widen(mixed_heads)), axis=2))
        delta_blocks = delta_rows.reshape(N_CTX, TOK_DEV, H).transpose(0, 2, 1)
        grad_blocks = grad_mixed.reshape(N_CTX, TOK_DEV, D)
        grad_pre = jnp.dot(grad_half, fc2_weight.T, preferred_element_type=jnp.float32) * gelu_slope(pre_act)
        grad_pre_half = grad_pre.astype(half_type)
        feedforward_hidden_gradient = jnp.dot(grad_pre_half, fc1_weight.T, preferred_element_type=jnp.float32)

        def attend_back(pair_grads, index):
            query_pos = index * TOK_DEV + offsets

            def visit(query_grad, other):
                key_pos = other * TOK_DEV + offsets

                def take(marker):
                    return block_backward(query_blocks[index], key_blocks[other], value_blocks[other], grad_blocks[index], log_totals[index], delta_blocks[index], query_pos, key_pos)

                def skip(marker):
                    blank = jnp.zeros((TOK_DEV, D), jnp.float32)
                    return (blank, blank, blank)
                parts = lax.cond(other <= index, take, skip, jnp.int32(0))
                return (query_grad + parts[0], (parts[1], parts[2]))
            query_grad, stacked = lax.scan(visit, jnp.zeros((TOK_DEV, D), jnp.float32), block_ids)
            return ((pair_grads[0] + stacked[0], pair_grads[1] + stacked[1]), query_grad)
        blank_all = jnp.zeros((N_CTX, TOK_DEV, D), jnp.float32)
        pair_final, query_grads = lax.scan(attend_back, (blank_all, blank_all), block_ids)
        grad_queries = unrotate_heads(split_heads(query_grads.reshape(LENGTH, D)), cos_table, sin_table).reshape(LENGTH, D)
        grad_keys = unrotate_heads(split_heads(pair_final[0].reshape(LENGTH, D)), cos_table, sin_table).reshape(LENGTH, D)
        grad_proj = jnp.concatenate([grad_queries, grad_keys, pair_final[1].reshape(LENGTH, D)], axis=1)
        grad_proj_half = grad_proj.astype(half_type)
        attention_hidden_gradient = jnp.dot(grad_proj_half, qkv_weight.T, preferred_element_type=jnp.float32)
        input_token_rows = gradient_token_rows + layernorm_backward(attention_hidden_gradient, attention_standardized, attention_inverse_spread, attention_norm_gain) + layernorm_backward(feedforward_hidden_gradient, feedforward_standardized, feedforward_inverse_spread, feedforward_norm_gain)
        gain_products_first = attention_hidden_gradient * attention_standardized
        gain_products_second = feedforward_hidden_gradient * feedforward_standardized

        def partial_sums(totals_in, index):

            def piece(array):
                return lax.dynamic_slice_in_dim(array, index * TOK_DEV, TOK_DEV, 0)
            terms = (lax.optimization_barrier(jnp.sum(piece(gain_products_first), axis=0)), lax.optimization_barrier(jnp.sum(piece(attention_hidden_gradient), axis=0)), lax.optimization_barrier(jnp.sum(piece(gain_products_second), axis=0)), lax.optimization_barrier(jnp.sum(piece(feedforward_hidden_gradient), axis=0)), jnp.dot(piece(hidden1).T, piece(grad_proj_half), preferred_element_type=jnp.float32), lax.optimization_barrier(jnp.sum(piece(grad_proj), axis=0)), jnp.dot(piece(mixed_heads).T, piece(grad_half), preferred_element_type=jnp.float32), lax.optimization_barrier(jnp.sum(piece(gradient_token_rows), axis=0)), jnp.dot(piece(hidden2).T, piece(grad_pre_half), preferred_element_type=jnp.float32), lax.optimization_barrier(jnp.sum(piece(grad_pre), axis=0)), jnp.dot(piece(activation).T, piece(grad_half), preferred_element_type=jnp.float32), lax.optimization_barrier(jnp.sum(piece(gradient_token_rows), axis=0)))
            return (tuple((total + widen(lax.optimization_barrier(term.astype(half_type))) for total, term in zip(totals_in, terms))), None)
        grad_sums, unused_sums = lax.scan(partial_sums, grad_sums, block_ids)
        return (grad_sums, (layer_rows, input_token_rows))
    start_sums = tuple((jnp.zeros(param.shape, jnp.float32) for param in params))
    grads, rows_out = lax.scan(sequence, start_sums, (layer_in, cotangent))
    return (rows_out[0], rows_out[1], grads[0], grads[1], grads[2], grads[3], grads[4], grads[5], grads[6], grads[7], grads[8], grads[9], grads[10], grads[11])
```

```python
import functools
import math

import jax
import jax.numpy as jnp
from jax import lax
from jax.experimental import pallas as pl
from jax.experimental.pallas import tpu as pltpu
from jax.sharding import PartitionSpec as P

H = 16
HD = 64
ROT = 16

norm_eps = 1e-05
masked_score = -1e30
root_half = 1.0 / math.sqrt(2.0)
root_two_pi = 1.0 / math.sqrt(2.0 * math.pi)
BF = jnp.bfloat16
F32 = jnp.float32
MESH = pl.DeviceIdType.MESH
VM = pl.BlockSpec(memory_space=pltpu.VMEM)


class Group:
    def __init__(self, name, F, C):
        self.name = name
        self.f = lax.axis_index("fsdp")
        self.c = lax.axis_index("ctx")
        if name == "fsdp":
            self.n, self.me = F, self.f
        elif name == "ctx":
            self.n, self.me = C, self.c
        elif name == "plane":
            self.n, self.me = C // 2, self.c // 2
        else:
            self.n, self.me = 2, lax.rem(self.c, 2)

    def peer(self, k):
        return lax.rem(self.me + k, self.n)

    def device(self, index):
        if self.name == "fsdp":
            return {"fsdp": index}
        if self.name == "ctx":
            return {"ctx": index}
        if self.name == "plane":
            return {"ctx": index * 2 + lax.rem(self.c, 2)}
        return {"ctx": (self.c // 2) * 2 + index}


GROUP_SIZE = {
    "fsdp": lambda F, C: F,
    "ctx": lambda F, C: C,
    "plane": lambda F, C: C // 2,
    "core": lambda F, C: 2,
}


def comm(cid, F, C, inputs, outputs, scratch, ops):
    names = list(inputs) + list(outputs) + list(scratch)
    sizes = [GROUP_SIZE[op[0]](F, C) for op in ops]
    offset = [sum(sizes[:i]) for i in range(len(ops))]
    total = sum(sizes)
    used = sorted({op[0] for op in ops})

    def kernel(*args):
        refs = dict(zip(names, args))
        send_sem, recv_sem = args[len(names)], args[len(names) + 1]
        groups = {u: Group(u, F, C) for u in used}
        barrier = pltpu.get_barrier_semaphore()
        count = 0
        for u in used:
            if u in ("plane", "core") and "ctx" in used:
                continue
            g = groups[u]
            for k in range(1, g.n):
                pl.semaphore_signal(
                    barrier, inc=1, device_id=g.device(g.peer(k)), device_id_type=MESH
                )
                count += 1
        pl.semaphore_wait(barrier, count)
        started = {}
        done = set()

        def finish(i):
            if i in done:
                return
            done.add(i)
            for copy in started[i]:
                copy.wait()

        for i, (gname, src_view, dst_view, own, after) in enumerate(ops):
            for j in after:
                finish(j)
            g = groups[gname]
            copies = []
            for k in range(1, g.n):
                peer = g.peer(k)
                copy = pltpu.make_async_remote_copy(
                    src_ref=src_view(refs, g, peer),
                    dst_ref=dst_view(refs, g),
                    send_sem=send_sem.at[offset[i] + k],
                    recv_sem=recv_sem.at[offset[i] + k],
                    device_id=g.device(peer),
                    device_id_type=MESH,
                )
                copy.start()
                copies.append(copy)
            if own:
                copy = pltpu.make_async_copy(
                    src_view(refs, g, g.me), dst_view(refs, g), send_sem.at[offset[i]]
                )
                copy.start()
                copies.append(copy)
            started[i] = copies
        for i in range(len(ops)):
            finish(i)

    result = pl.pallas_call(
        kernel,
        name="comm%d" % cid,
        out_shape=[jax.ShapeDtypeStruct(s, d) for s, d in outputs.values()],
        in_specs=[VM] * len(inputs),
        out_specs=[VM] * len(outputs),
        scratch_shapes=[pltpu.VMEM(s, d) for s, d in scratch.values()]
        + [pltpu.SemaphoreType.DMA((total,)), pltpu.SemaphoreType.DMA((total,))],
        compiler_params=pltpu.CompilerParams(
            collective_id=cid, has_side_effects=True, vmem_limit_bytes=60 * 2**20
        ),
    )(*inputs.values())
    return dict(zip(outputs, result))


def op_all_to_all(group, src, dst, after=()):
    return (group, lambda r, g, p: r[src].at[p], lambda r, g: r[dst].at[g.me], True, after)


def op_gather(group, src, dst, after=()):
    return (group, lambda r, g, p: r[src], lambda r, g: r[dst].at[g.me], True, after)


def attention_kernel(in_ref, cos_ref, sa_ref, sb_ref, out_ref, dk_ref, dv_ref, dq_ref):
    length, CH = in_ref.shape[1:]
    rows = min(256, length)
    dk_ref[...] = jnp.zeros_like(dk_ref)
    dv_ref[...] = jnp.zeros_like(dv_ref)
    lane = lax.broadcasted_iota(jnp.int32, (rows, CH), 1)
    masks = [(lane >= h * HD) & (lane < (h + 1) * HD) for h in range(CH // HD)]

    def nt(a, b):
        return lax.dot_general(a, b, (((1,), (1,)), ((), ())), preferred_element_type=F32)

    def tn(a, b):
        return lax.dot_general(a, b, (((0,), (0,)), ((), ())), preferred_element_type=F32)

    for i in range(length // rows):
        lo, hi = i * rows, (i + 1) * rows
        q = in_ref[0, lo:hi, :] * jnp.asarray(HD**-0.5, BF)
        g = in_ref[3, lo:hi, :]
        k = in_ref[1, :hi, :]
        v = in_ref[2, :hi, :]
        visible = lo + lax.broadcasted_iota(
            jnp.int32, (rows, hi), 0
        ) >= lax.broadcasted_iota(jnp.int32, (rows, hi), 1)
        mixed = None
        dq = None
        for h in range(CH // HD):
            qm = jnp.where(masks[h], q, jnp.zeros_like(q))
            gm = jnp.where(masks[h], g, jnp.zeros_like(g))
            s = jnp.where(visible, nt(qm, k), masked_score)
            p = jnp.exp(s - jnp.max(s, axis=1, keepdims=True))
            inv = 1.0 / jnp.sum(p, axis=1, keepdims=True)
            o = (jnp.dot(p.astype(BF), v, preferred_element_type=F32) * inv).astype(BF)
            delta = jnp.sum(gm.astype(F32) * o.astype(F32), axis=1, keepdims=True)
            probs = p * inv
            dv_ref[:hi, :] += tn(probs.astype(BF), gm)
            ds = (probs * (nt(gm, v) - delta)).astype(BF)
            dk_ref[:hi, :] += tn(ds, qm)
            dqh = jnp.dot(ds, k, preferred_element_type=F32)
            mixed = o if h == 0 else jnp.where(masks[h], o, mixed)
            dq = dqh if h == 0 else jnp.where(masks[h], dqh, dq)
        out_ref[0, lo:hi, :] = mixed
        dq_ref[lo:hi, :] = dq * HD**-0.5

    def unrotate(x):
        left = pltpu.roll(x, CH - ROT // 2, 1)
        right = pltpu.roll(x, ROT // 2, 1)
        return x * cos_ref[...] - left * sa_ref[...] - right * sb_ref[...]

    out_ref[1] = unrotate(dq_ref[...]).astype(BF)
    out_ref[2] = unrotate(dk_ref[...]).astype(BF)
    out_ref[3] = dv_ref[...].astype(BF)


def attention(stack, tables):
    length, CH = stack.shape[1:]
    return pl.pallas_call(
        attention_kernel,
        name="attention",
        out_shape=jax.ShapeDtypeStruct((4, length, CH), BF),
        in_specs=[VM] * 4,
        out_specs=VM,
        scratch_shapes=[pltpu.VMEM((length, CH), F32)] * 3,
        compiler_params=pltpu.CompilerParams(vmem_limit_bytes=60 * 2**20),
    )(stack, *tables)


def rotary_tables(positions, width):
    half = ROT // 2
    freqs = jnp.power(10000.0, -2.0 * jnp.arange(half, dtype=F32) / ROT)
    angles = positions.astype(F32)[:, None] * freqs[None, :]
    c, s = jnp.cos(angles), jnp.sin(angles)
    n = positions.shape[0]
    rest = HD - ROT
    zero = jnp.zeros((n, half), F32)
    cos_t = jnp.concatenate([c, c, jnp.ones((n, rest), F32)], axis=1)
    sa = jnp.concatenate([-s, zero, jnp.zeros((n, rest), F32)], axis=1)
    sb = jnp.concatenate([zero, s, jnp.zeros((n, rest), F32)], axis=1)
    return tuple(jnp.tile(t, (1, width // HD)) for t in (cos_t, sa, sb))


def dot(a, b):
    return jnp.dot(a, b, preferred_element_type=F32)


def dot_nt(a, b):
    return lax.dot_general(a, b, (((1,), (1,)), ((), ())), preferred_element_type=F32)


def dot_tn(a, b):
    return lax.dot_general(a, b, (((0,), (0,)), ((), ())), preferred_element_type=F32)


def on_device(
    F,
    C,
    layer_in,
    ln1_gain,
    ln1_bias,
    ln2_gain,
    ln2_bias,
    qkv_weight,
    qkv_bias,
    out_weight,
    out_bias,
    fc1_weight,
    fc1_bias,
    fc2_weight,
    fc2_bias,
    cotangent,
):
    x = layer_in[0]
    cot = cotangent[0]
    T, D = x.shape
    FF = fc1_weight.shape[1]
    DF, FFF = D // F, FF // F
    R = D // (F * C)
    RF = FF // (F * C)
    PN = C // 2
    f_index = lax.axis_index("fsdp")
    c_index = lax.axis_index("ctx")
    N = F * T
    WC = 3 * DF + FFF
    CH = D // C

    centered = x - jnp.mean(x, axis=1, keepdims=True)
    inv_scale = lax.rsqrt(jnp.mean(centered * centered, axis=1, keepdims=True) + norm_eps)
    xhat = centered * inv_scale

    q_rows = lax.dynamic_slice_in_dim(qkv_weight, c_index * R, R, 0)
    f_rows = lax.dynamic_slice_in_dim(fc1_weight, c_index * R, R, 0)
    w_send = jnp.concatenate(
        [
            q_rows.reshape(R, 3, F, DF).transpose(2, 0, 1, 3).reshape(F, R, 3 * DF),
            f_rows.reshape(R, F, FFF).transpose(1, 0, 2),
        ],
        axis=2,
    )
    small = jnp.concatenate(
        [ln1_gain, ln1_bias, ln2_gain, ln2_bias, out_bias, fc2_bias, qkv_bias]
    ).astype(F32)
    small_rows = -(-small.shape[0] // 1024) * 8
    small_in = jnp.pad(small, (0, small_rows * 128 - small.shape[0])).reshape(small_rows, 128)
    got = comm(
        1,
        F,
        C,
        {"w": w_send, "small": small_in, "xh": xhat.astype(BF), "gh": cot.astype(BF)},
        {
            "xa": ((F, T, D), BF),
            "ga": ((F, T, D), BF),
            "sa": ((F, small_rows, 128), F32),
            "wf": ((F, PN, 2, R, WC), BF),
        },
        {"wt": ((F, R, WC), BF)},
        [
            op_all_to_all("fsdp", "w", "wt"),
            op_gather("fsdp", "small", "sa"),
            op_gather("fsdp", "xh", "xa"),
            op_gather("fsdp", "gh", "ga"),
            (
                "plane",
                lambda r, g, p: r["wt"],
                lambda r, g: r["wf"].at[:, g.me, lax.rem(g.c, 2)],
                True,
                (0,),
            ),
            (
                "core",
                lambda r, g, p: r["wf"].at[:, :, g.me],
                lambda r, g: r["wf"].at[:, :, g.me],
                False,
                (4,),
            ),
        ],
    )
    w_all = got["wf"].reshape(D, WC)
    w_qkv = w_all[:, : 3 * DF]
    w_fc1 = w_all[:, 3 * DF :]
    small_all = got["sa"].reshape(F, small_rows * 128)
    vec = [small_all[:, i * DF : (i + 1) * DF].reshape(D) for i in range(6)]
    gain1, bias1, gain2, bias2, b_out, b_fc2 = vec
    b_qkv = small_all[:, 6 * DF : 9 * DF].reshape(3, F, DF)
    b_qkv = lax.dynamic_slice_in_dim(b_qkv, f_index, 1, 1).reshape(3 * DF)
    xh = got["xa"].reshape(N, D).astype(F32)
    gh = got["ga"].reshape(N, D)
    hidden1 = (xh * gain1 + bias1).astype(BF)
    hidden2 = (xh * gain2 + bias2).astype(BF)

    proj = dot(hidden1, w_qkv) + b_qkv
    positions = c_index * T + jnp.arange(T, dtype=jnp.int32)
    tables = rotary_tables(positions, 2 * DF)
    cos_t, sa_t, sb_t = (jnp.tile(t, (F, 1)) for t in tables)
    qk = proj[:, : 2 * DF]
    half = ROT // 2
    qk = qk * cos_t + jnp.roll(qk, -half, 1) * sa_t + jnp.roll(qk, half, 1) * sb_t
    grad_mixed = dot_nt(gh, out_weight).astype(BF)
    stack = jnp.concatenate(
        [qk.astype(BF), proj[:, 2 * DF :].astype(BF), grad_mixed], axis=1
    )
    pairs = DF // CH
    stack = stack.reshape(F, T, 4, pairs, CH).transpose(0, 3, 2, 1, 4).reshape(C, 4, T, CH)
    spread = comm(
        2,
        F,
        C,
        {"s": stack},
        {"d": ((4, C, T, CH), BF)},
        {},
        [("ctx", lambda r, g, p: r["s"].at[p], lambda r, g: r["d"].at[:, g.me], True, ())],
    )["d"]
    length_tables = rotary_tables(jnp.arange(C * T, dtype=jnp.int32), CH)
    heads = attention(spread.reshape(4, C * T, CH), length_tables)
    back = comm(
        3,
        F,
        C,
        {"s": heads.reshape(4, C, T, CH)},
        {"d": ((4, C, T, CH), BF)},
        {},
        [("ctx", lambda r, g, p: r["s"].at[:, p], lambda r, g: r["d"].at[:, g.me], True, ())],
    )["d"]
    back = back.reshape(4, F, pairs, T, CH).transpose(1, 3, 0, 2, 4).reshape(N, 4 * DF)
    mixed = back[:, :DF]
    grad_proj = back[:, DF:]

    pre_act = dot(hidden2, w_fc1) + fc1_bias.astype(F32)
    cdf = 0.5 * (1.0 + lax.erf(pre_act * root_half))
    activation = (pre_act * cdf).astype(BF)
    slope = cdf + pre_act * jnp.exp(-0.5 * pre_act * pre_act) * root_two_pi
    grad_pre = dot_nt(gh, fc2_weight) * slope
    grad_pre_half = grad_pre.astype(BF)
    grad_hidden2 = dot_nt(grad_pre_half, w_fc1)
    grad_hidden1 = dot_nt(grad_proj, w_qkv)

    y_part = dot(activation, fc2_weight) + dot(mixed, out_weight)
    g_part = grad_hidden1 * gain1 + grad_hidden2 * gain2
    yg = jnp.stack(
        [y_part.astype(BF).reshape(F, T, D), g_part.astype(BF).reshape(F, T, D)], axis=1
    )

    g_fc1 = dot_tn(hidden2, grad_pre_half).astype(BF).reshape(F, PN, 2, R, FFF)
    g_qkv = dot_tn(hidden1, grad_proj).astype(BF).reshape(F, PN, 2, R, 3 * DF)
    g_fc2 = dot_tn(activation, gh).astype(BF).reshape(PN, 2, RF, D)
    g_out = dot_tn(mixed, gh).astype(BF).reshape(PN, 2, R, D)
    cot_sum = jnp.sum(cot, axis=0)
    qkv_sum = jnp.sum(grad_proj.astype(F32), axis=0).reshape(3, 1, DF)
    mine = jnp.arange(F)[None, :, None] == f_index
    fc1_sum = jnp.sum(grad_pre, axis=0)
    mine_fc1 = jnp.arange(F)[:, None] == f_index
    vec_sums = jnp.concatenate(
        [
            jnp.sum(grad_hidden1 * xh, axis=0),
            jnp.sum(grad_hidden1, axis=0),
            jnp.sum(grad_hidden2 * xh, axis=0),
            jnp.sum(grad_hidden2, axis=0),
            cot_sum,
            jnp.where(mine, qkv_sum, 0.0).reshape(3 * D),
            jnp.where(mine_fc1, fc1_sum[None], 0.0).reshape(FF),
        ]
    )
    vec_total = lax.psum(vec_sums, ("ctx", "fsdp"))

    def other_core(name, wide):
        if wide:
            src = lambda r, g, p: r[name].at[:, :, p]
        else:
            src = lambda r, g, p: r[name].at[:, p]
        return ("core", src, lambda r, g: r[name + "_o"], False, ())

    got = comm(
        4,
        F,
        C,
        {"yg": yg, "fc1": g_fc1, "qkv": g_qkv, "fc2": g_fc2, "out": g_out},
        {
            "yga": ((F, 2, T, D), BF),
            "fc1_o": ((F, PN, R, FFF), BF),
            "qkv_o": ((F, PN, R, 3 * DF), BF),
            "fc2_o": ((PN, RF, D), BF),
            "out_o": ((PN, R, D), BF),
        },
        {},
        [
            op_all_to_all("fsdp", "yg", "yga"),
            other_core("fc1", True),
            other_core("qkv", True),
            other_core("fc2", False),
            other_core("out", False),
        ],
    )
    yg_sum = jnp.sum(got["yga"].astype(F32), axis=0)
    layer_rows = x + yg_sum[0] + (b_out + b_fc2)
    g = yg_sum[1]
    in_rows = cot + inv_scale * (
        g
        - jnp.mean(g, axis=1, keepdims=True)
        - xhat * jnp.mean(g * xhat, axis=1, keepdims=True)
    )

    core = lax.rem(c_index, 2)

    def own_core(array, axis):
        part = lax.dynamic_slice_in_dim(array, core, 1, axis)
        return lax.squeeze(part, (axis,))

    def add(a, b):
        return (a.astype(F32) + b.astype(F32)).astype(BF)

    h_fc1 = add(own_core(g_fc1, 2), got["fc1_o"]).transpose(1, 0, 2, 3)
    h_qkv = add(own_core(g_qkv, 2), got["qkv_o"]).transpose(1, 0, 2, 3)
    h_fc2 = add(own_core(g_fc2, 1), got["fc2_o"])
    h_out = add(own_core(g_out, 1), got["out_o"])
    halves = {"fc1": h_fc1, "qkv": h_qkv, "fc2": h_fc2, "out": h_out}
    got = comm(
        5,
        F,
        C,
        halves,
        {n + "_o": (a.shape, BF) for n, a in halves.items()},
        {},
        [op_all_to_all("plane", n, n + "_o") for n in halves],
    )
    red = {n: jnp.sum(got[n + "_o"].astype(F32), axis=0).astype(BF) for n in halves}

    def spread_core(name, number):
        view = lambda r, g: r[name].at[:, g.me]
        return ("core", lambda r, g, p: view(r, g), view, False, (number,))

    def spread_plane(src, name, after):
        return (
            "plane",
            lambda r, g, p: r[src],
            lambda r, g: r[name].at[g.me, lax.rem(g.c, 2)],
            True,
            after,
        )

    got = comm(
        6,
        F,
        C,
        red,
        {
            "fc1_o": ((PN, 2, F, R, FFF), BF),
            "qkv_o": ((PN, 2, F, R, 3 * DF), BF),
            "fc2_o": ((PN, 2, RF, D), BF),
            "out_o": ((PN, 2, R, D), BF),
        },
        {"fc1_t": ((F, R, FFF), BF), "qkv_t": ((F, R, 3 * DF), BF)},
        [
            op_all_to_all("fsdp", "fc1", "fc1_t"),
            op_all_to_all("fsdp", "qkv", "qkv_t"),
            spread_plane("fc2", "fc2_o", ()),
            spread_plane("out", "out_o", ()),
            spread_plane("fc1_t", "fc1_o", (0,)),
            spread_plane("qkv_t", "qkv_o", (1,)),
            spread_core("fc2_o", 2),
            spread_core("out_o", 3),
            spread_core("fc1_o", 4),
            spread_core("qkv_o", 5),
        ],
    )
    d_fc1 = (
        got["fc1_o"].reshape(C, F, R, FFF).transpose(0, 2, 1, 3).reshape(DF, FF).astype(F32)
    )
    d_qkv = (
        got["qkv_o"]
        .reshape(C, F, R, 3, DF)
        .transpose(0, 2, 3, 1, 4)
        .reshape(DF, 3 * D)
        .astype(F32)
    )
    d_fc2 = got["fc2_o"].reshape(FFF, D).astype(F32)
    d_out = got["out_o"].reshape(DF, D).astype(F32)

    def own_part(start, size):
        return lax.dynamic_slice_in_dim(
            vec_total[start : start + size], f_index * (size // F), size // F, 0
        )

    cot_total = own_part(4 * D, D)
    return (
        layer_rows[None],
        in_rows[None],
        own_part(0, D),
        own_part(D, D),
        own_part(2 * D, D),
        own_part(3 * D, D),
        d_qkv,
        own_part(5 * D, 3 * D),
        d_out,
        cot_total,
        d_fc1,
        own_part(8 * D, FF),
        d_fc2,
        cot_total,
    )


def solution(mesh):
    F, C = mesh.shape["fsdp"], mesh.shape["ctx"]
    rows, row, mat = P("fsdp", "ctx", None), P("fsdp"), P("fsdp", None)
    return jax.shard_map(
        functools.partial(on_device, F, C),
        mesh=mesh,
        in_specs=(rows, row, row, row, row, mat, row, mat, row, mat, row, mat, row, rows),
        out_specs=(rows, rows, row, row, row, row, mat, row, mat, row, mat, row, mat, row),
        check_vma=False,
    )
```

```python
import functools
import math

import jax
import jax.numpy as jnp
from jax import lax
from jax.experimental import pallas as pl
from jax.experimental.pallas import tpu as pltpu
from jax.sharding import PartitionSpec as P

H = 16
HD = 64
ROT = 16

norm_eps = 1e-05
masked_score = -1e30
root_half = 1.0 / math.sqrt(2.0)
root_two_pi = 1.0 / math.sqrt(2.0 * math.pi)
BF = jnp.bfloat16
F32 = jnp.float32
MESH = pl.DeviceIdType.MESH
VM = pl.BlockSpec(memory_space=pltpu.VMEM)


class Group:
    def __init__(self, name, F, C):
        self.name = name
        self.f = lax.axis_index("fsdp")
        self.c = lax.axis_index("ctx")
        if name == "fsdp":
            self.n, self.me = F, self.f
        elif name == "ctx":
            self.n, self.me = C, self.c
        elif name == "plane":
            self.n, self.me = C // 2, self.c // 2
        else:
            self.n, self.me = 2, lax.rem(self.c, 2)

    def peer(self, k):
        return lax.rem(self.me + k, self.n)

    def device(self, index):
        if self.name == "fsdp":
            return {"fsdp": index}
        if self.name == "ctx":
            return {"ctx": index}
        if self.name == "plane":
            return {"ctx": index * 2 + lax.rem(self.c, 2)}
        return {"ctx": (self.c // 2) * 2 + index}


GROUP_SIZE = {
    "fsdp": lambda F, C: F,
    "ctx": lambda F, C: C,
    "plane": lambda F, C: C // 2,
    "core": lambda F, C: 2,
}


def comm(cid, F, C, inputs, outputs, scratch, ops, relays=()):
    names = list(inputs) + list(outputs) + list(scratch)
    sizes = [GROUP_SIZE[op[0]](F, C) if op[0] else 0 for op in ops]
    offset = [sum(sizes[:i]) for i in range(len(ops))]
    relay_at = sum(sizes)
    steps = F - 1
    total = relay_at + len(relays) * (2 * steps + 1)
    used = sorted({op[0] for op in ops if op[0]})

    def kernel(*args):
        refs = dict(zip(names, args))
        send_sem, recv_sem = args[len(names)], args[len(names) + 1]
        groups = {u: Group(u, F, C) for u in used}
        barrier = pltpu.get_barrier_semaphore()
        count = 0
        for u in used:
            if u in ("plane", "core") and "ctx" in used:
                continue
            g = groups[u]
            for k in range(1, g.n):
                pl.semaphore_signal(
                    barrier, inc=1, device_id=g.device(g.peer(k)), device_id_type=MESH
                )
                count += 1
        pl.semaphore_wait(barrier, count)
        started = {}
        done = set()

        def relay_copy(i, way, t, index):
            src, dst = relays[i]
            slot = relay_at + (2 * i + (way > 0)) * steps + t
            f = groups["fsdp"].f
            return pltpu.make_async_remote_copy(
                src_ref=refs[src] if t == 0 else refs[dst].at[index],
                dst_ref=refs[dst].at[index],
                send_sem=send_sem.at[slot],
                recv_sem=recv_sem.at[slot],
                device_id={"fsdp": lax.rem(f + way + F, F)},
                device_id_type=MESH,
            )

        def relay_sends(way, t):
            f = groups["fsdp"].f
            source, target = f - way * t, f + way
            return source, (source >= 0) & (source < F) & (target >= 0) & (target < F)

        def relay_start(t):
            for i in range(len(relays)):
                for way in (1, -1):
                    source, go = relay_sends(way, t)

                    @pl.when(go)
                    def _():
                        relay_copy(i, way, t, source).start()

        def relay_receive(t):
            for i in range(len(relays)):
                for way in (1, -1):
                    source = groups["fsdp"].f - way * (t + 1)

                    @pl.when((source >= 0) & (source < F))
                    def _():
                        relay_copy(i, way, t, source).wait_recv()

        def relay_own(i):
            src, dst = relays[i]
            return pltpu.make_async_copy(
                refs[src], refs[dst].at[groups["fsdp"].f], send_sem.at[total - 1 - i]
            )

        def relay_begin():
            relay_start(0)
            for i in range(len(relays)):
                relay_own(i).start()

        def relay_rest():
            for t in range(steps):
                relay_receive(t)
                if t + 1 < steps:
                    relay_start(t + 1)
            for i in range(len(relays)):
                relay_own(i).wait()
                for way in (1, -1):
                    for t in range(steps):
                        source, go = relay_sends(way, t)

                        @pl.when(go)
                        def _():
                            relay_copy(i, way, t, source).wait_send()

        def finish(i):
            if i in done:
                return
            done.add(i)
            for copy in started[i]:
                copy.wait()

        relay_state = 0
        for i, (gname, src_view, dst_view, own, after) in enumerate(ops):
            if relays and after and relay_state == 0:
                relay_begin()
                relay_state = 1
            for j in after:
                finish(j)
            if relays and relay_state == 1 and any(ops[j][4] for j in after):
                relay_rest()
                relay_state = 2
            if gname is None:
                src_view(refs, groups)
                started[i] = []
                continue
            g = groups[gname]
            copies = []
            for k in range(1, g.n):
                peer = g.peer(k)
                copy = pltpu.make_async_remote_copy(
                    src_ref=src_view(refs, g, peer),
                    dst_ref=dst_view(refs, g),
                    send_sem=send_sem.at[offset[i] + k],
                    recv_sem=recv_sem.at[offset[i] + k],
                    device_id=g.device(peer),
                    device_id_type=MESH,
                )
                copy.start()
                copies.append(copy)
            if own:
                copy = pltpu.make_async_copy(
                    src_view(refs, g, g.me), dst_view(refs, g), send_sem.at[offset[i]]
                )
                copy.start()
                copies.append(copy)
            started[i] = copies
        if relays and relay_state == 0:
            relay_begin()
        if relays and relay_state < 2:
            relay_rest()
        for i in range(len(ops)):
            finish(i)

    result = pl.pallas_call(
        kernel,
        name="comm%d" % cid,
        out_shape=[jax.ShapeDtypeStruct(s, d) for s, d in outputs.values()],
        in_specs=[VM] * len(inputs),
        out_specs=[VM] * len(outputs),
        scratch_shapes=[pltpu.VMEM(s, d) for s, d in scratch.values()]
        + [pltpu.SemaphoreType.DMA((total,)), pltpu.SemaphoreType.DMA((total,))],
        compiler_params=pltpu.CompilerParams(
            collective_id=cid, has_side_effects=True, vmem_limit_bytes=60 * 2**20
        ),
    )(*inputs.values())
    return dict(zip(outputs, result))


def op_all_to_all(group, src, dst, after=()):
    return (group, lambda r, g, p: r[src].at[p], lambda r, g: r[dst].at[g.me], True, after)


def op_gather(group, src, dst, after=()):
    return (group, lambda r, g, p: r[src], lambda r, g: r[dst].at[g.me], True, after)


def attention_kernel(in_ref, cos_ref, sa_ref, sb_ref, out_ref, dk_ref, dv_ref, dq_ref):
    length, CH = in_ref.shape[1:]
    rows = min(256, length)
    dk_ref[...] = jnp.zeros_like(dk_ref)
    dv_ref[...] = jnp.zeros_like(dv_ref)
    lane = lax.broadcasted_iota(jnp.int32, (rows, CH), 1)
    masks = [(lane >= h * HD) & (lane < (h + 1) * HD) for h in range(CH // HD)]

    def nt(a, b):
        return lax.dot_general(a, b, (((1,), (1,)), ((), ())), preferred_element_type=F32)

    def tn(a, b):
        return lax.dot_general(a, b, (((0,), (0,)), ((), ())), preferred_element_type=F32)

    for i in range(length // rows):
        lo, hi = i * rows, (i + 1) * rows
        q = in_ref[0, lo:hi, :] * jnp.asarray(HD**-0.5, BF)
        g = in_ref[3, lo:hi, :]
        k = in_ref[1, :hi, :]
        v = in_ref[2, :hi, :]
        visible = lo + lax.broadcasted_iota(
            jnp.int32, (rows, hi), 0
        ) >= lax.broadcasted_iota(jnp.int32, (rows, hi), 1)
        mixed = None
        dq = None
        for h in range(CH // HD):
            qm = jnp.where(masks[h], q, jnp.zeros_like(q))
            gm = jnp.where(masks[h], g, jnp.zeros_like(g))
            s = jnp.where(visible, nt(qm, k), masked_score)
            p = jnp.exp(s - jnp.max(s, axis=1, keepdims=True))
            inv = 1.0 / jnp.sum(p, axis=1, keepdims=True)
            o = (jnp.dot(p.astype(BF), v, preferred_element_type=F32) * inv).astype(BF)
            delta = jnp.sum(gm.astype(F32) * o.astype(F32), axis=1, keepdims=True)
            probs = p * inv
            dv_ref[:hi, :] += tn(probs.astype(BF), gm)
            ds = (probs * (nt(gm, v) - delta)).astype(BF)
            dk_ref[:hi, :] += tn(ds, qm)
            dqh = jnp.dot(ds, k, preferred_element_type=F32)
            mixed = o if h == 0 else jnp.where(masks[h], o, mixed)
            dq = dqh if h == 0 else jnp.where(masks[h], dqh, dq)
        out_ref[0, lo:hi, :] = mixed
        dq_ref[lo:hi, :] = dq * HD**-0.5

    def unrotate(x):
        left = pltpu.roll(x, CH - ROT // 2, 1)
        right = pltpu.roll(x, ROT // 2, 1)
        return x * cos_ref[...] - left * sa_ref[...] - right * sb_ref[...]

    out_ref[1] = unrotate(dq_ref[...]).astype(BF)
    out_ref[2] = unrotate(dk_ref[...]).astype(BF)
    out_ref[3] = dv_ref[...].astype(BF)


def attention(stack, tables):
    length, CH = stack.shape[1:]
    return pl.pallas_call(
        attention_kernel,
        name="attention",
        out_shape=jax.ShapeDtypeStruct((4, length, CH), BF),
        in_specs=[VM] * 4,
        out_specs=VM,
        scratch_shapes=[pltpu.VMEM((length, CH), F32)] * 3,
        compiler_params=pltpu.CompilerParams(vmem_limit_bytes=60 * 2**20),
    )(stack, *tables)


def rotary_tables(positions, width):
    half = ROT // 2
    freqs = jnp.power(10000.0, -2.0 * jnp.arange(half, dtype=F32) / ROT)
    angles = positions.astype(F32)[:, None] * freqs[None, :]
    c, s = jnp.cos(angles), jnp.sin(angles)
    n = positions.shape[0]
    rest = HD - ROT
    zero = jnp.zeros((n, half), F32)
    cos_t = jnp.concatenate([c, c, jnp.ones((n, rest), F32)], axis=1)
    sa = jnp.concatenate([-s, zero, jnp.zeros((n, rest), F32)], axis=1)
    sb = jnp.concatenate([zero, s, jnp.zeros((n, rest), F32)], axis=1)
    return tuple(jnp.tile(t, (1, width // HD)) for t in (cos_t, sa, sb))


def dot(a, b):
    return jnp.dot(a, b, preferred_element_type=F32)


def dot_nt(a, b):
    return lax.dot_general(a, b, (((1,), (1,)), ((), ())), preferred_element_type=F32)


def dot_tn(a, b):
    return lax.dot_general(a, b, (((0,), (0,)), ((), ())), preferred_element_type=F32)


def on_device(
    F,
    C,
    layer_in,
    ln1_gain,
    ln1_bias,
    ln2_gain,
    ln2_bias,
    qkv_weight,
    qkv_bias,
    out_weight,
    out_bias,
    fc1_weight,
    fc1_bias,
    fc2_weight,
    fc2_bias,
    cotangent,
):
    x = layer_in[0]
    cot = cotangent[0]
    T, D = x.shape
    FF = fc1_weight.shape[1]
    DF, FFF = D // F, FF // F
    R = D // (F * C)
    RF = FF // (F * C)
    PN = C // 2
    f_index = lax.axis_index("fsdp")
    c_index = lax.axis_index("ctx")
    N = F * T
    WC = 3 * DF + FFF
    CH = D // C

    centered = x - jnp.mean(x, axis=1, keepdims=True)
    inv_scale = lax.rsqrt(jnp.mean(centered * centered, axis=1, keepdims=True) + norm_eps)
    xhat = centered * inv_scale

    def send_columns(name, stride, width, j, at):
        return (
            "fsdp",
            lambda r, g, p: r[name].at[
                g.c, :, pl.ds(pl.multiple_of(j * stride + p * width, 128), width)
            ],
            lambda r, g: r["wt"].at[g.me, :, pl.ds(at, width)],
            True,
            (),
        )

    small = jnp.concatenate(
        [ln1_gain, ln1_bias, ln2_gain, ln2_bias, out_bias, fc2_bias, qkv_bias]
    ).astype(F32)
    small_rows = -(-small.shape[0] // 1024) * 8
    small_in = jnp.pad(small, (0, small_rows * 128 - small.shape[0])).reshape(small_rows, 128)
    got = comm(
        1,
        F,
        C,
        {
            "qkv": qkv_weight.reshape(C, R, 3 * D),
            "fc1": fc1_weight.reshape(C, R, FF),
            "small": small_in,
            "xh": xhat.astype(BF),
            "gh": cot.astype(BF),
        },
        {
            "xa": ((F, T, D), BF),
            "ga": ((F, T, D), BF),
            "sa": ((F, small_rows, 128), F32),
            "wf": ((F, PN, 2, R, WC), BF),
        },
        {"wt": ((F, R, WC), BF)},
        [
            send_columns("qkv", D, DF, 0, 0),
            send_columns("qkv", D, DF, 1, DF),
            send_columns("qkv", D, DF, 2, 2 * DF),
            send_columns("fc1", 0, FFF, 0, 3 * DF),
            op_gather("fsdp", "small", "sa"),
            (
                "plane",
                lambda r, g, p: r["wt"],
                lambda r, g: r["wf"].at[:, g.me, lax.rem(g.c, 2)],
                True,
                (0, 1, 2, 3),
            ),
            (
                "core",
                lambda r, g, p: r["wf"].at[:, :, g.me],
                lambda r, g: r["wf"].at[:, :, g.me],
                False,
                (5,),
            ),
        ],
        [("xh", "xa"), ("gh", "ga")],
    )
    w_all = got["wf"].reshape(D, WC)
    w_qkv = w_all[:, : 3 * DF]
    w_fc1 = w_all[:, 3 * DF :]
    small_all = got["sa"].reshape(F, small_rows * 128)
    vec = [small_all[:, i * DF : (i + 1) * DF].reshape(D) for i in range(6)]
    gain1, bias1, gain2, bias2, b_out, b_fc2 = vec
    b_qkv = small_all[:, 6 * DF : 9 * DF].reshape(3, F, DF)
    b_qkv = lax.dynamic_slice_in_dim(b_qkv, f_index, 1, 1).reshape(3 * DF)
    xh = got["xa"].reshape(N, D).astype(F32)
    gh = got["ga"].reshape(N, D)
    hidden1 = (xh * gain1 + bias1).astype(BF)
    hidden2 = (xh * gain2 + bias2).astype(BF)

    pre_act = dot(hidden2, w_fc1) + fc1_bias.astype(F32)
    cdf = 0.5 * (1.0 + lax.erf(pre_act * root_half))
    activation = (pre_act * cdf).astype(BF)
    slope = cdf + pre_act * jnp.exp(-0.5 * pre_act * pre_act) * root_two_pi
    grad_pre = dot_nt(gh, fc2_weight) * slope
    grad_pre_half = grad_pre.astype(BF)
    grad_hidden2 = dot_nt(grad_pre_half, w_fc1)
    g_fc1 = dot_tn(hidden2, grad_pre_half).astype(BF).reshape(F, PN, 2, R, FFF)
    g_fc2 = dot_tn(activation, gh).astype(BF).reshape(PN, 2, RF, D)
    y_ff = dot(activation, fc2_weight)

    core = lax.rem(c_index, 2)

    def own_core(array, axis):
        part = lax.dynamic_slice_in_dim(array, core, 1, axis)
        return lax.squeeze(part, (axis,))

    def add(a, b):
        return (a.astype(F32) + b.astype(F32)).astype(BF)

    def other_core(name, wide):
        if wide:
            src = lambda r, g, p: r[name].at[:, :, p]
        else:
            src = lambda r, g, p: r[name].at[:, p]
        return ("core", src, lambda r, g: r[name + "_o"], False, ())

    proj = dot(hidden1, w_qkv) + b_qkv
    positions = c_index * T + jnp.arange(T, dtype=jnp.int32)
    tables = rotary_tables(positions, 2 * DF)
    cos_t, sa_t, sb_t = (jnp.tile(t, (F, 1)) for t in tables)
    qk = proj[:, : 2 * DF]
    half = ROT // 2
    qk = qk * cos_t + jnp.roll(qk, -half, 1) * sa_t + jnp.roll(qk, half, 1) * sb_t
    grad_mixed = dot_nt(gh, out_weight).astype(BF)
    stack = jnp.concatenate(
        [qk.astype(BF), proj[:, 2 * DF :].astype(BF), grad_mixed], axis=1
    )
    pairs = DF // CH
    stack = stack.reshape(F, T, 4, pairs, CH).transpose(0, 3, 2, 1, 4).reshape(C, 4, T, CH)
    got = comm(
        2,
        F,
        C,
        {"s": stack, "fc1": g_fc1, "fc2": g_fc2},
        {
            "d": ((4, C, T, CH), BF),
            "fc1_o": ((F, PN, R, FFF), BF),
            "fc2_o": ((PN, RF, D), BF),
        },
        {},
        [
            ("ctx", lambda r, g, p: r["s"].at[p], lambda r, g: r["d"].at[:, g.me], True, ()),
            other_core("fc1", True),
            other_core("fc2", False),
        ],
    )
    spread = got["d"]
    h_fc1 = add(own_core(g_fc1, 2), got["fc1_o"]).transpose(1, 0, 2, 3)
    h_fc2 = add(own_core(g_fc2, 1), got["fc2_o"])
    length_tables = rotary_tables(jnp.arange(C * T, dtype=jnp.int32), CH)
    heads = attention(spread.reshape(4, C * T, CH), length_tables)
    back = comm(
        3,
        F,
        C,
        {"s": heads.reshape(4, C, T, CH)},
        {"d": ((4, C, T, CH), BF)},
        {},
        [("ctx", lambda r, g, p: r["s"].at[:, p], lambda r, g: r["d"].at[:, g.me], True, ())],
    )["d"]
    back = back.reshape(4, F, pairs, T, CH).transpose(1, 3, 0, 2, 4).reshape(N, 4 * DF)
    mixed = back[:, :DF]
    grad_proj = back[:, DF:]

    grad_hidden1 = dot_nt(grad_proj, w_qkv)

    y_part = y_ff + dot(mixed, out_weight)
    g_part = grad_hidden1 * gain1 + grad_hidden2 * gain2
    yg = jnp.stack(
        [y_part.astype(BF).reshape(F, T, D), g_part.astype(BF).reshape(F, T, D)], axis=1
    )

    g_qkv = dot_tn(hidden1, grad_proj).astype(BF).reshape(F, PN, 2, R, 3 * DF)
    g_out = dot_tn(mixed, gh).astype(BF).reshape(PN, 2, R, D)
    cot_sum = jnp.sum(cot, axis=0)
    qkv_sum = jnp.sum(grad_proj.astype(F32), axis=0).reshape(3, 1, DF)
    mine = jnp.arange(F)[None, :, None] == f_index
    fc1_sum = jnp.sum(grad_pre, axis=0)
    mine_fc1 = jnp.arange(F)[:, None] == f_index
    vec_sums = jnp.concatenate(
        [
            jnp.sum(grad_hidden1 * xh, axis=0).reshape(F, DF),
            jnp.sum(grad_hidden1, axis=0).reshape(F, DF),
            jnp.sum(grad_hidden2 * xh, axis=0).reshape(F, DF),
            jnp.sum(grad_hidden2, axis=0).reshape(F, DF),
            cot_sum.reshape(F, DF),
            jnp.where(mine, qkv_sum, 0.0).reshape(F, 3 * DF),
            jnp.where(mine_fc1, fc1_sum[None], 0.0),
        ],
        axis=1,
    )
    VR = -(-vec_sums.shape[1] // 1024) * 8
    vec_sums = jnp.pad(vec_sums, ((0, 0), (0, VR * 128 - vec_sums.shape[1])))

    def sum_cores(r, groups):
        own = groups["core"].me
        for i in range(PN):
            r["qkv_h"][i] = (
                r["qkv"][:, i, own].astype(F32) + r["qkv_i"][:, i].astype(F32)
            ).astype(BF)
        for i in range(PN):
            r["out_h"][i] = (r["out"][i, own].astype(F32) + r["out_i"][i].astype(F32)).astype(BF)

    def into(name, dst):
        if name == "qkv":
            src = lambda r, g, p: r[name].at[:, :, p]
        else:
            src = lambda r, g, p: r[name].at[:, p]
        return ("core", src, lambda r, g: r[dst], False, ())

    got = comm(
        4,
        F,
        C,
        {
            "yg": yg,
            "vec": vec_sums.reshape(F, VR, 128),
            "qkv": g_qkv,
            "out": g_out,
            "fc1_h": h_fc1,
            "fc2_h": h_fc2,
        },
        {
            "yga": ((F, 2, T, D), BF),
            "vec_o": ((F, VR, 128), F32),
            "fc1_o": ((PN, F, R, FFF), BF),
            "fc2_o": ((PN, RF, D), BF),
            "qkv_o": ((PN, F, R, 3 * DF), BF),
            "out_o": ((PN, R, D), BF),
        },
        {
            "qkv_i": ((F, PN, R, 3 * DF), BF),
            "out_i": ((PN, R, D), BF),
            "qkv_h": ((PN, F, R, 3 * DF), BF),
            "out_h": ((PN, R, D), BF),
        },
        [
            into("qkv", "qkv_i"),
            into("out", "out_i"),
            op_all_to_all("fsdp", "vec", "vec_o"),
            op_all_to_all("fsdp", "yg", "yga"),
            op_all_to_all("plane", "fc1_h", "fc1_o"),
            op_all_to_all("plane", "fc2_h", "fc2_o"),
            (None, sum_cores, None, False, (0, 1)),
            op_all_to_all("plane", "qkv_h", "qkv_o"),
            op_all_to_all("plane", "out_h", "out_o"),
        ],
    )
    yg_sum = jnp.sum(got["yga"].astype(F32), axis=0)
    layer_rows = x + yg_sum[0] + (b_out + b_fc2)
    g = yg_sum[1]
    in_rows = cot + inv_scale * (
        g
        - jnp.mean(g, axis=1, keepdims=True)
        - xhat * jnp.mean(g * xhat, axis=1, keepdims=True)
    )

    names = ("fc1", "qkv", "fc2", "out")
    vec_own = jnp.sum(got["vec_o"], axis=0)
    red = {n: jnp.sum(got[n + "_o"].astype(F32), axis=0).astype(BF) for n in names}

    def spread_core(name, number):
        view = lambda r, g: r[name].at[:, g.me]
        return ("core", lambda r, g, p: view(r, g), view, False, (number,))

    def spread_plane(src, name, after):
        return (
            "plane",
            lambda r, g, p: r[src],
            lambda r, g: r[name].at[g.me, lax.rem(g.c, 2)],
            True,
            after,
        )

    def to_columns(name, dst, stride, width, j):
        return (
            "fsdp",
            lambda r, g, p: r[name].at[p, :, pl.ds(j * width, width)],
            lambda r, g: r[dst].at[
                :, pl.ds(pl.multiple_of(j * stride + g.me * width, 128), width)
            ],
            True,
            (),
        )

    got = comm(
        6,
        F,
        C,
        {**red, "vec": vec_own},
        {
            "fc1_o": ((PN, 2, R, FF), BF),
            "qkv_o": ((PN, 2, R, 3 * D), BF),
            "fc2_o": ((PN, 2, RF, D), BF),
            "out_o": ((PN, 2, R, D), BF),
            "vec_o": ((C, VR, 128), F32),
        },
        {"fc1_t": ((R, FF), BF), "qkv_t": ((R, 3 * D), BF)},
        [
            op_gather("ctx", "vec", "vec_o"),
            to_columns("fc1", "fc1_t", 0, FFF, 0),
            to_columns("qkv", "qkv_t", D, DF, 0),
            to_columns("qkv", "qkv_t", D, DF, 1),
            to_columns("qkv", "qkv_t", D, DF, 2),
            spread_plane("fc2", "fc2_o", ()),
            spread_plane("out", "out_o", ()),
            spread_plane("fc1_t", "fc1_o", (1,)),
            spread_plane("qkv_t", "qkv_o", (2, 3, 4)),
            spread_core("fc2_o", 5),
            spread_core("out_o", 6),
            spread_core("fc1_o", 7),
            spread_core("qkv_o", 8),
        ],
    )
    d_fc1 = got["fc1_o"].reshape(DF, FF).astype(F32)
    d_qkv = got["qkv_o"].reshape(DF, 3 * D).astype(F32)
    d_fc2 = got["fc2_o"].reshape(FFF, D).astype(F32)
    d_out = got["out_o"].reshape(DF, D).astype(F32)
    vec_total = jnp.sum(got["vec_o"], axis=0).reshape(VR * 128)

    def own_part(start, size):
        return vec_total[start * DF : start * DF + size]

    cot_total = own_part(4, DF)
    return (
        layer_rows[None],
        in_rows[None],
        own_part(0, DF),
        own_part(1, DF),
        own_part(2, DF),
        own_part(3, DF),
        d_qkv,
        own_part(5, 3 * DF),
        d_out,
        cot_total,
        d_fc1,
        own_part(8, FFF),
        d_fc2,
        cot_total,
    )


def solution(mesh):
    F, C = mesh.shape["fsdp"], mesh.shape["ctx"]
    rows, row, mat = P("fsdp", "ctx", None), P("fsdp"), P("fsdp", None)
    return jax.shard_map(
        functools.partial(on_device, F, C),
        mesh=mesh,
        in_specs=(rows, row, row, row, row, mat, row, mat, row, mat, row, mat, row, rows),
        out_specs=(rows, rows, row, row, row, row, mat, row, mat, row, mat, row, mat, row),
        check_vma=False,
    )
```
